32 devices in a mesh: dp: 8 (over y, x, core), seq: 4 (over z).
Axes of the slice: x: 2, y: 2, z: 4, core: 2. Of those that a mesh axis runs over, the one named last changes fastest.
Arguments:
- queries: bfloat16 [16, 256, 5120], P('dp', 'seq'), may hold values from -50 to 50
- key_rows: bfloat16 [16, 256, 1024], P('dp', 'seq'), may hold values from -6 to 6
- value_rows: bfloat16 [16, 256, 1024], P('dp', 'seq'), may hold values from -6 to 6
- cotangent: bfloat16 [16, 256, 5120], P('dp', 'seq'), may hold values from -6 to 6
- episodes: int32 [16, 256], P('dp', 'seq'), may hold values from 0 to 7, never falling along the last dimension, each value on 1 to 170 neighbouring positions
- send_slot: int32 [8], P('dp'), may hold values from 0 to 1
- swap_mask: int32 [1], replicated, may hold values from 1 to 7
Outputs:
- grad_queries: bfloat16 [16, 256, 5120], P('dp', 'seq')
- grad_keys: bfloat16 [16, 256, 1024], P('dp', 'seq')
- grad_values: bfloat16 [16, 256, 1024], P('dp', 'seq')
The draws below stay inside these ranges and needn't reach their ends.
Inputs may be any that keep to these rules, and one draw needn't show every extreme that they name: `episodes`: episode ids never fall along a span.
All inputs are finite; a program needn't handle non-finite values.
Results may differ from the reference program's by a relative error of at most 0.0055.
Values may be sent and summed in bfloat16 or wider, within the bound.
A program may use at most 64 MiB of HBM per device.

```python
import math
import jax
import jax.numpy as jnp
import numpy as np
from jax import lax

H = 40
KVH = 8
DH = 128
SPANS = 2
EPIS = 8
SPAN_LEN = 256
MOST = 170
ALL_SPANS = 16
N_DP = 8


def paired_draw(key):
    first, second = jax.random.split(jax.random.fold_in(key, 17), 2)
    groups = H // KVH
    query_part = jnp.clip(jax.random.normal(first, (ALL_SPANS, SPAN_LEN, KVH, groups, DH), jnp.float32), -6.0, 6.0)
    key_part = jnp.clip(jax.random.normal(second, (ALL_SPANS, SPAN_LEN, KVH, DH), jnp.float32), -6.0, 6.0)
    return (query_part.reshape(ALL_SPANS, SPAN_LEN, H * DH), key_part.reshape(ALL_SPANS, SPAN_LEN, KVH * DH))


def draw_queries(key, part):
    return paired_draw(key)[0].astype(jnp.bfloat16)


def draw_key_rows(key, part):
    return paired_draw(key)[1].astype(jnp.bfloat16)


def set_ends(values, rng, low, top_value):
    longest = values.shape.index(max(values.shape))
    spots = []
    for shift in (0, 1):
        where = [jax.random.randint(jax.random.fold_in(rng, axis), (), 0, length) for axis, length in enumerate(values.shape)]
        where[longest] = (where[longest] + shift) % values.shape[longest]
        spots.append(tuple(where))
    return values.at[spots[0]].set(low).at[spots[1]].set(top_value)


def level_of(key, shape, pieces, least, high):
    def one(dim, shards_of):
        steps = jax.random.uniform(jax.random.fold_in(jax.random.fold_in(key, 6), dim), (shards_of,), jnp.float32, least / len(pieces), high / len(pieces))
        return jnp.repeat(jnp.exp(steps), shape[dim] // shards_of).reshape((-1,) + (1,) * (len(shape) - dim - 1))

    loudness = one(*pieces[0])
    for cut in pieces[1:]:
        loudness = loudness * one(*cut)
    return loudness


def split_up(count, total, limit, slope):
    portions = [(1 << 20) // math.isqrt(standing ** slope) + 1 for standing in range(2, count + 1)]
    surplus, given = total - limit - (count - 1), [1] * (count - 1)
    while surplus > 0:
        movable = [i for i in range(count - 1) if given[i] < limit]
        pool, left = sum([portions[i] for i in movable]), surplus
        for i in movable:
            more = min(limit - given[i], max(1, left * portions[i] // pool), surplus)
            given[i] = given[i] + more
            surplus = surplus - more
    return np.array([limit] + given)


def ragged(rng, count, total, reach, lean):
    if count == 2:
        one = jax.random.randint(rng, (), max(1, total - reach), min(reach, total - 1) + 1)
        return jnp.stack([one, total - one])
    tallies = jnp.asarray(split_up(count, total, reach, lean), jnp.int32)
    couples = (count - 1) // 2
    donor, receiver = tallies[1:1 + 2 * couples:2], tallies[2:2 + 2 * couples:2]
    room = jnp.minimum(donor - 1, reach - receiver)
    moved = jax.random.randint(jax.random.fold_in(rng, 1), (couples,), 0, 1 << 20) % (room + 1)
    tallies = tallies.at[1:1 + 2 * couples:2].set(donor - moved).at[2:2 + 2 * couples:2].set(receiver + moved)
    return tallies[jax.random.permutation(jax.random.fold_in(rng, 2), count)]


def bell_draw(own_key, extent, deviation, bound, pieces=(), held_as=jnp.bfloat16):
    loudness = level_of(own_key, extent, pieces, -0.22, 0.18) if pieces else 1.0
    values = jax.random.normal(own_key, extent, jnp.float32) * deviation * loudness
    return jnp.minimum(jnp.maximum(values, -bound), bound).astype(held_as)


def setup_inputs(seed: int = 0) -> dict:
    key_list = jax.random.split(jax.random.key(seed), 8)
    return {
        "queries": draw_queries(jax.random.fold_in(key_list[7], 71), 0),
        "key_rows": draw_key_rows(jax.random.fold_in(key_list[7], 71), 0),
        "value_rows": bell_draw(key_list[2], (ALL_SPANS, SPAN_LEN, KVH * DH), 1.0, 6.0, ((0, 8), (1, 4))),
        "cotangent": bell_draw(key_list[3], (ALL_SPANS, SPAN_LEN, H * DH), 1.0, 6.0, ((0, 8), (1, 4))),
        "episodes": jax.vmap(lambda own: jnp.searchsorted(jnp.cumsum(ragged(own, EPIS, SPAN_LEN, MOST, 2)), jnp.arange(SPAN_LEN), side="right"))(jax.random.split(key_list[4], ALL_SPANS)).reshape((ALL_SPANS, SPAN_LEN)).astype(jnp.int32),
        "send_slot": set_ends(jax.random.randint(key_list[5], (N_DP,), 0, 2), jax.random.fold_in(key_list[5], 1), 0, 1).astype(jnp.int32),
        "swap_mask": jax.random.randint(key_list[6], (1,), 1, N_DP).astype(jnp.int32),
    }


def head_group(query_group, key_head, value_head, grad_group, episode_ids):
    scaling = 1.0 / jnp.sqrt(jnp.float32(DH))
    query_full = query_group.astype(jnp.float32)
    key_full = key_head.astype(jnp.float32)
    value_full = value_head.astype(jnp.float32)
    grad_full = grad_group.astype(jnp.float32)
    scores = jnp.einsum('qgd,td->gqt', query_full, key_full) * scaling
    positions = jnp.arange(SPAN_LEN, dtype=jnp.int32)
    allowed = (episode_ids[:, None] == episode_ids[None, :]) & (positions[:, None] >= positions[None, :])
    scores = jnp.where(allowed[None], scores, jnp.float32(-1e+30))
    top = lax.optimization_barrier(jnp.max(scores, axis=-1, keepdims=True))
    expo = jnp.exp(scores - top)
    probs = expo / lax.optimization_barrier(jnp.sum(expo, axis=-1, keepdims=True))
    probs_low = lax.optimization_barrier(probs.astype(jnp.bfloat16)).astype(jnp.float32)
    dprobs = jnp.einsum('qgd,td->gqt', grad_full, value_full)
    delta = lax.optimization_barrier(jnp.sum(probs * dprobs, axis=-1, keepdims=True))
    dscores = lax.optimization_barrier((probs * (dprobs - delta)).astype(jnp.bfloat16)).astype(jnp.float32)
    grad_value = jnp.einsum('gqt,qgd->td', probs_low, grad_full).astype(jnp.bfloat16)
    grad_query = (jnp.einsum('gqt,td->qgd', dscores, key_full) * scaling).astype(jnp.bfloat16)
    grad_key = (jnp.einsum('gqt,qgd->td', dscores, query_full) * scaling).astype(jnp.bfloat16)
    return (grad_query, grad_key, grad_value)

def span_grads(packed):
    query_span, key_span, value_span, grad_span, episode_ids = packed
    groups = H // KVH
    query_heads = query_span.reshape(SPAN_LEN, KVH, groups, DH).transpose(1, 0, 2, 3)
    grad_heads = grad_span.reshape(SPAN_LEN, KVH, groups, DH).transpose(1, 0, 2, 3)
    key_heads = key_span.reshape(SPAN_LEN, KVH, DH).transpose(1, 0, 2)
    value_heads = value_span.reshape(SPAN_LEN, KVH, DH).transpose(1, 0, 2)

    def per_head(packed_group):
        return head_group(packed_group[0], packed_group[1], packed_group[2], packed_group[3], episode_ids)
    grad_query, grad_key, grad_value = lax.map(per_head, (query_heads, key_heads, value_heads, grad_heads))
    grad_query = grad_query.transpose(1, 0, 2, 3).reshape(SPAN_LEN, H * DH)
    grad_key = grad_key.transpose(1, 0, 2).reshape(SPAN_LEN, KVH * DH)
    grad_value = grad_value.transpose(1, 0, 2).reshape(SPAN_LEN, KVH * DH)
    return (grad_query, grad_key, grad_value)

def reference(queries, key_rows, value_rows, cotangent, episodes, send_slot, swap_mask):
    grad_query, grad_key, grad_value = lax.map(span_grads, (queries, key_rows, value_rows, cotangent, episodes))
    replicas = jnp.arange(N_DP, dtype=jnp.int32)
    partner = jnp.bitwise_xor(replicas, swap_mask[0]).astype(jnp.int32)
    kept_index = replicas * SPANS + 1 - send_slot
    taken_index = partner * SPANS + send_slot[partner]
    order = jnp.stack([kept_index, taken_index], axis=1).reshape(-1).astype(jnp.int32)
    return (grad_query[order], grad_key[order], grad_value[order])
```

```python
import functools

import jax
import jax.numpy as jnp
from jax import lax
from jax.experimental import pallas as pl
from jax.experimental.pallas import tpu as pltpu
from jax.sharding import PartitionSpec as P

DH = 128
LEAD_TOP = 7
LEAD = 2
LAG = 7
DIRECT = 3
MESH = pl.DeviceIdType.MESH
NT = (((1,), (1,)), ((), ()))
NN = (((1,), (0,)), ((), ()))
TN = (((0,), (0,)), ((), ()))


def dot(a, b, dims):
    return lax.dot_general(a, b, dims, preferred_element_type=jnp.float32)


def kernel(
    n, ndp, mask, send_ref, ep_ref, q_hbm, k_hbm, v_hbm, do_hbm,
    gq_out, gk_out, gv_out,
    q_ref, k_ref, v_ref, do_ref, load_sem, keep_sem, kvbuf, epbuf, allow, gpart, gown, grecv, tq, tk, tv,
    own_send, own_recv, fwd_send, fwd_recv, ep_send, ep_recv, acc_send, acc_recv, down_send, down_recv,
    trade_send, trade_recv,
):
    r = lax.axis_index("dp")
    s = lax.axis_index("seq")
    rows = q_ref.shape[1]
    heads = k_ref.shape[2] // DH
    groups = q_ref.shape[2] // k_ref.shape[2]
    pieces = 2 * heads
    direct = min(DIRECT, heads)
    summed = pieces - direct
    wide = groups * rows
    scaling = 1.0 / jnp.sqrt(jnp.float32(DH))
    partner = r
    for b in range(ndp.bit_length() - 1):
        if (mask >> b) & 1:
            partner = partner + (1 << b) * (1 - 2 * ((r // (1 << b)) % 2))
    handed = send_ref[0]
    most = 2 * n * rows // 3

    def first(d):
        return min(max(0, d * rows - most + 1) // 16 * 16, rows)

    def low(k):
        return max(0, (k + 1) * rows - most + 1) // 16 * 16

    reach = [d for d in range(1, n) if first(d) < rows]
    own = pl.ds(pl.multiple_of(s * rows, rows), rows)
    top = (n - 1) * rows
    above = (s + 1) % n

    def slot(c):
        return handed + c * (1 - 2 * handed)

    barrier = pltpu.get_barrier_semaphore()

    @pl.when(s > 0)
    def _():
        pl.semaphore_signal(barrier, inc=1, device_id=(r, (s + n - 1) % n), device_id_type=MESH)

    pl.semaphore_signal(barrier, inc=1, device_id=(partner, s), device_id_type=MESH)
    loads = [
        pltpu.make_async_copy(src, dst, load_sem.at[i])
        for i, (src, dst) in enumerate(
            ((k_hbm, k_ref), (v_hbm, v_ref), (q_hbm, q_ref), (do_hbm, do_ref))
        )
    ]
    for load in loads:
        load.start()
    loads[0].wait()
    loads[1].wait()

    for c in range(2):
        epbuf[s, c:c + 1, 0:rows] = jnp.where(
            slot(c) == 0, ep_ref[0:1, :], ep_ref[1:2, :]
        )
        for g in range(heads):
            kvbuf[c, g, own, 0:DH] = k_ref[slot(c), :, g * DH:(g + 1) * DH]
            kvbuf[c, g, own, DH:2 * DH] = v_ref[slot(c), :, g * DH:(g + 1) * DH]

    @pl.when(s < n - 1)
    def _():
        pl.semaphore_wait(barrier, 2)

    @pl.when(s == n - 1)
    def _():
        pl.semaphore_wait(barrier, 1)

    def chunk(t, skip=0):
        return pl.ds(pl.multiple_of(t * rows + skip, 16), rows - skip)

    def up_own(p, t):
        part = kvbuf.at[p // heads, p % heads, chunk(t), :]
        return pltpu.make_async_remote_copy(
            src_ref=part, dst_ref=part, send_sem=own_send, recv_sem=own_recv.at[p],
            device_id=(r, above), device_id_type=MESH,
        )

    def up_fwd(p, k):
        part = kvbuf.at[p // heads, p % heads, pl.ds(low(k), k * rows - low(k)), :]
        return pltpu.make_async_remote_copy(
            src_ref=part, dst_ref=part, send_sem=fwd_send, recv_sem=fwd_recv.at[p],
            device_id=(r, above), device_id_type=MESH,
        )

    def ep_copy(t):
        return pltpu.make_async_remote_copy(
            src_ref=epbuf.at[t], dst_ref=epbuf.at[t],
            send_sem=ep_send.at[t], recv_sem=ep_recv.at[t],
            device_id=(r, above), device_id_type=MESH,
        )

    def down_sum(p):
        part = (p // heads, p % heads, pl.ds(low(n - 2), top - low(n - 2)))
        return pltpu.make_async_remote_copy(
            src_ref=gpart.at[part], dst_ref=grecv.at[part],
            send_sem=acc_send.at[p // heads], recv_sem=acc_recv.at[p],
            device_id=(r, (s + n - 1) % n), device_id_type=MESH,
        )

    def down(p, d):
        c, g = p // heads, p % heads
        return pltpu.make_async_remote_copy(
            src_ref=gpart.at[c, g, chunk((s + n - d) % n, first(d))],
            dst_ref=grecv.at[c, g, chunk(s, first(d))],
            send_sem=down_send.at[d], recv_sem=down_recv.at[p, s],
            device_id=(r, (s + n - d) % n), device_id_type=MESH,
        )

    def down_arrival(p, d):
        c, g = p // heads, p % heads
        part = grecv.at[c, g, chunk((s + d) % n, first(d))]
        return pltpu.make_async_remote_copy(
            src_ref=part, dst_ref=part,
            send_sem=down_send.at[d], recv_sem=down_recv.at[p, (s + d) % n],
            device_id=(r, (s + d) % n), device_id_type=MESH,
        )

    def send_down(p):
        for d in reversed(reach):
            @pl.when(s >= d)
            def _(d=d):
                down(p, d).start()

    def trade(which, g, buf, out, width):
        cols = pl.ds(pl.multiple_of(g * width, width), width)
        return pltpu.make_async_remote_copy(
            src_ref=buf.at[0, :, cols], dst_ref=out.at[1, :, cols],
            send_sem=trade_send.at[which], recv_sem=trade_recv.at[which],
            device_id=(partner, s), device_id_type=MESH,
        )

    def keep(which, g, buf, out, width):
        cols = pl.ds(pl.multiple_of(g * width, width), width)
        return pltpu.make_async_copy(
            buf.at[1, :, cols], out.at[0, :, cols], keep_sem.at[which]
        )

    def send_own(p):
        @pl.when((s < n - 1) & (p < pieces))
        def _():
            up_own(p, s).start()

    lead = jnp.where(s == n - 2, LEAD_TOP, LEAD)

    @pl.when(s < n - 1)
    def _():
        ep_copy(s).start()

        def early(p, carry):
            up_own(p, s).start()
            return carry

        lax.fori_loop(0, lead, early, 0)

    def clear(at, size):
        def one(i, carry):
            kvbuf[i // heads, i % heads, pl.ds(at, size), :] = (
                jnp.zeros((size, 2 * DH), jnp.bfloat16)
            )
            return carry

        lax.fori_loop(0, 2 * heads, one, 0)

    eye = lax.broadcasted_iota(jnp.int32, (rows, DH), 0) == lax.broadcasted_iota(
        jnp.int32, (rows, DH), 1
    )

    def see(t):
        def one(c, carry):
            mine = epbuf[s, pl.ds(c, 1), 0:rows]
            mine = jnp.concatenate([mine] * groups, axis=1)
            pos_q = jnp.concatenate(
                [s * rows + lax.broadcasted_iota(jnp.int32, (rows, rows), 1)] * groups, axis=1
            )
            line = epbuf[t, pl.ds(c, 1), :]
            column = jnp.sum(jnp.where(eye, line, 0), axis=1, keepdims=True)
            pos_k = t * rows + lax.broadcasted_iota(jnp.int32, (rows, wide), 0)
            seen = jnp.where(pos_k <= pos_q, 1.0, 0.0) * jnp.where(column == mine, 1.0, 0.0)
            allow[c, chunk(t), :] = seen
            return carry

        lax.fori_loop(0, 2, one, 0)

    for t in range(n):
        @pl.when(t > s)
        def _(t=t):
            clear(t * rows, rows)
            for c in range(2):
                allow[c, t * rows:(t + 1) * rows, :] = jnp.zeros((rows, wide), jnp.float32)
    for k in range(1, n):
        if low(k - 1) > 0:
            @pl.when(s == k)
            def _(k=k):
                clear(0, low(k - 1))
    see(s)
    loads[2].wait()
    loads[3].wait()

    def ep_step(d, carry):
        t = s - d
        ep_copy(t).wait_recv()

        @pl.when(s < n - 1)
        def _():
            ep_copy(t).start()
        see(t)
        return carry

    lax.fori_loop(1, s + 1, ep_step, 0)

    def forward(p):
        @pl.when(s > 0)
        def _():
            up_own(p, (s + n - 1) % n).wait_recv()
        for k in range(1, n):
            @pl.when(s == k)
            def _(k=k):
                if k > 1:
                    up_fwd(p, k - 1).wait_recv()
                if k < n - 1:
                    up_fwd(p, k).start()

    def compute(p):
        c, g = p // heads, p % heads
        at = slot(c)

        def stack(ref):
            return jnp.concatenate(
                [
                    ref[at, :, pl.ds(pl.multiple_of((g * groups + i) * DH, DH), DH)]
                    for i in range(groups)
                ],
                axis=0,
            )

        q = stack(q_ref)
        do = stack(do_ref)
        key = kvbuf[c, g, :, 0:DH]
        value = kvbuf[c, g, :, DH:2 * DH]
        scores = jnp.where(allow[c] > 0.5, dot(key, q, NT) * scaling, jnp.float32(-1e30))
        peak = jnp.max(scores, axis=0, keepdims=True)
        expo = jnp.exp(scores - peak)
        probs = expo * (1.0 / jnp.sum(expo, axis=0, keepdims=True))
        dprobs = dot(value, do, NT)
        delta = jnp.sum(probs * dprobs, axis=0, keepdims=True)
        dscores = (probs * (dprobs - delta)).astype(jnp.bfloat16)
        gk = dot(dscores, q, NN)
        gv = dot(probs.astype(jnp.bfloat16), do, NN)
        gown[c, g, :, 0:DH] = gk
        gown[c, g, :, DH:2 * DH] = gv
        gpart[c, g, :, 0:DH] = gk.astype(jnp.bfloat16)
        gpart[c, g, :, DH:2 * DH] = gv.astype(jnp.bfloat16)

        @pl.when((s == n - 1) & (p < summed))
        def _():
            down_sum(p).start()

        @pl.when((s < n - 2) | (p >= summed))
        def _():
            send_down(p)

        gq = (dot(dscores, key, TN) * scaling).astype(jnp.bfloat16)
        for i in range(groups):
            cols = pl.ds(pl.multiple_of((g * groups + i) * DH, DH), DH)
            tq[c, :, cols] = gq[i * rows:(i + 1) * rows]

        @pl.when(c == 0)
        def _():
            trade(0, g, tq, gq_out, groups * DH).start()

        @pl.when(c == 1)
        def _():
            keep(0, g, tq, gq_out, groups * DH).start()

    def finish(p):
        c, g = p // heads, p % heads

        @pl.when((s == n - 2) & (p < summed))
        def _():
            part = (c, g, pl.ds(low(n - 2), top - low(n - 2)))
            down_sum(p).wait_recv()
            total = gown[part] + grecv[part].astype(jnp.float32)
            gown[part] = total
            gpart[part] = total.astype(jnp.bfloat16)
            send_down(p)

        for d in reach:
            @pl.when((s + d < n - 1) | ((s + d == n - 1) & (p >= summed)))
            def _(d=d):
                down_arrival(p, d).wait_recv()
                part = (c, g, chunk(s, first(d)))
                gown[part] += grecv[c, g, chunk(s + d, first(d))].astype(jnp.float32)

        cols = pl.ds(pl.multiple_of(g * DH, DH), DH)
        tk[c, :, cols] = (gown[c, g, own, 0:DH] * scaling).astype(jnp.bfloat16)
        tv[c, :, cols] = gown[c, g, own, DH:2 * DH].astype(jnp.bfloat16)

        @pl.when(c == 0)
        def _():
            trade(1, g, tk, gk_out, DH).start()
            trade(2, g, tv, gv_out, DH).start()

        @pl.when(c == 1)
        def _():
            keep(1, g, tk, gk_out, DH).start()
            keep(2, g, tv, gv_out, DH).start()

    late = jnp.where(s == n - 1, 0, jnp.where(s == n - 2, LAG, pieces))

    def step(i, carry):
        send_own(i + lead)

        @pl.when(i < pieces)
        def _():
            forward(i)
            compute(i)

        @pl.when(i >= late)
        def _():
            finish(i - late)
        return carry

    lax.fori_loop(0, pieces + late, step, 0)

    def sent(part, sem):
        pltpu.make_async_remote_copy(
            src_ref=part, dst_ref=part, send_sem=sem, recv_sem=sem,
            device_id=(r, above), device_id_type=MESH,
        ).wait_send()

    @pl.when(s < n - 1)
    def _():
        sent(kvbuf.at[:, :, own, :], own_send)

        def one(t, carry):
            ep_copy(t).wait_send()
            return carry

        lax.fori_loop(0, s + 1, one, 0)

    for k in range(1, n - 1):
        @pl.when(s == k)
        def _(k=k):
            sent(kvbuf.at[:, :, pl.ds(low(k), k * rows - low(k)), :], fwd_send)

    for d in reach:
        @pl.when((s >= d) & (s < n - 1))
        def _(d=d):
            sent(gpart.at[:, :, chunk(s - d, first(d))], down_send.at[d])

    @pl.when(s == n - 1)
    def _():
        rest = pl.ds(low(n - 2), top - low(n - 2))
        sent(gpart.at[0, :, rest], acc_send.at[0])
        if summed > heads:
            sent(gpart.at[1, 0:summed - heads, rest], acc_send.at[1])
        for d in reach:
            sent(gpart.at[1, heads - direct:heads, chunk(s - d, first(d))], down_send.at[d])

    for which, buf, out in ((0, tq, gq_out), (1, tk, gk_out), (2, tv, gv_out)):
        pltpu.make_async_remote_copy(
            src_ref=buf.at[0], dst_ref=out.at[1],
            send_sem=trade_send.at[which], recv_sem=trade_recv.at[which],
            device_id=(partner, s), device_id_type=MESH,
        ).wait()
        pltpu.make_async_copy(buf.at[1], out.at[0], keep_sem.at[which]).wait()


def call(n, ndp, mask, send_slot, episodes, queries, key_rows, value_rows, cotangent):
    rows = queries.shape[1]
    heads = key_rows.shape[2] // DH
    groups = queries.shape[2] // key_rows.shape[2]
    pieces = 2 * heads
    vmem = pl.BlockSpec(memory_space=pltpu.VMEM)
    dma = pltpu.SemaphoreType.DMA
    return pl.pallas_call(
        functools.partial(kernel, n, ndp, mask),
        out_shape=[
            jax.ShapeDtypeStruct(x.shape, x.dtype) for x in (queries, key_rows, value_rows)
        ],
        in_specs=[pl.BlockSpec(memory_space=pltpu.SMEM), vmem]
        + [pl.BlockSpec(memory_space=pl.ANY)] * 4,
        out_specs=[pl.BlockSpec(memory_space=pl.ANY)] * 3,
        scratch_shapes=[
            pltpu.VMEM(queries.shape, jnp.bfloat16),
            pltpu.VMEM(key_rows.shape, jnp.bfloat16),
            pltpu.VMEM(value_rows.shape, jnp.bfloat16),
            pltpu.VMEM(cotangent.shape, jnp.bfloat16),
            dma((4,)),
            dma((3,)),
            pltpu.VMEM((2, heads, n * rows, 2 * DH), jnp.bfloat16),
            pltpu.VMEM((n, 8, DH), jnp.int32),
            pltpu.VMEM((2, n * rows, groups * rows), jnp.float32),
            pltpu.VMEM((2, heads, n * rows, 2 * DH), jnp.bfloat16),
            pltpu.VMEM((2, heads, n * rows, 2 * DH), jnp.float32),
            pltpu.VMEM((2, heads, n * rows, 2 * DH), jnp.bfloat16),
            pltpu.VMEM(queries.shape, jnp.bfloat16),
            pltpu.VMEM(key_rows.shape, jnp.bfloat16),
            pltpu.VMEM(value_rows.shape, jnp.bfloat16),
            dma,
            dma((pieces,)),
            dma,
            dma((pieces,)),
            dma((n,)),
            dma((n,)),
            dma((2,)),
            dma((pieces,)),
            dma((n,)),
            dma((pieces, n)),
            dma((3,)),
            dma((3,)),
        ],
        compiler_params=pltpu.CompilerParams(
            collective_id=mask, has_side_effects=True, vmem_limit_bytes=48 << 20
        ),
    )(send_slot, episodes, queries, key_rows, value_rows, cotangent)


def solution(mesh):
    n, ndp = mesh.shape["seq"], mesh.shape["dp"]

    def per_device(queries, key_rows, value_rows, cotangent, episodes, send_slot, swap_mask):
        return tuple(lax.switch(
            swap_mask[0] - 1,
            [functools.partial(call, n, ndp, mask) for mask in range(1, ndp)],
            send_slot, episodes, queries, key_rows, value_rows, cotangent,
        ))

    in_specs = (
        P("dp", "seq", None),
        P("dp", "seq", None),
        P("dp", "seq", None),
        P("dp", "seq", None),
        P("dp", "seq"),
        P("dp"),
        P(),
    )
    out_specs = (P("dp", "seq", None), P("dp", "seq", None), P("dp", "seq", None))
    return jax.shard_map(
        per_device, mesh=mesh, in_specs=in_specs, out_specs=out_specs, check_vma=False
    )
```

```python
import functools

import jax
import jax.numpy as jnp
from jax import lax
from jax.experimental import pallas as pl
from jax.experimental.pallas import tpu as pltpu
from jax.sharding import PartitionSpec as P

DH = 128
LEAD_TOP = 5
LEAD = 3
LAG = 5
BACK = 6
BACK_TOP = 1
DIRECT = 1
SOON = 2
TAIL_AT = 6
SOON_AT = 1
MESH = pl.DeviceIdType.MESH
NT = (((1,), (1,)), ((), ()))
NN = (((1,), (0,)), ((), ()))
TN = (((0,), (0,)), ((), ()))


def dot(a, b, dims):
    return lax.dot_general(a, b, dims, preferred_element_type=jnp.float32)


def kernel(
    n, ndp, mask, send_ref, ep_ref, q_hbm, k_hbm, v_hbm, do_hbm,
    gq_out, gk_out, gv_out,
    q_ref, k_ref, v_ref, do_ref, load_sem, keep_sem, kvbuf, epbuf, allow, gpart, gown, grecv, tq, tk, tv,
    far, far_send, far_recv, own_send, own_recv, fwd_send, fwd_recv, ep_send, ep_recv, acc_send, acc_recv, down_send, down_recv,
    trade_send, trade_recv,
):
    r = lax.axis_index("dp")
    s = lax.axis_index("seq")
    rows = q_ref.shape[1]
    heads = k_ref.shape[2] // DH
    groups = q_ref.shape[2] // k_ref.shape[2]
    pieces = 2 * heads
    direct = min(DIRECT, heads)
    soon = min(SOON, heads)
    wide = groups * rows
    scaling = 1.0 / jnp.sqrt(jnp.float32(DH))
    partner = r
    for b in range(ndp.bit_length() - 1):
        if (mask >> b) & 1:
            partner = partner + (1 << b) * (1 - 2 * ((r // (1 << b)) % 2))
    handed = send_ref[0]
    most = 2 * n * rows // 3

    def first(d):
        return min(max(0, d * rows - most + 1) // 16 * 16, rows)

    def low(k):
        return max(0, (k + 1) * rows - most + 1) // 16 * 16

    reach = [d for d in range(1, n) if first(d) < rows]
    own = pl.ds(pl.multiple_of(s * rows, rows), rows)
    top = (n - 1) * rows
    above = (s + 1) % n

    def summed(p):
        return (p >= soon) & (p < pieces - direct)

    middle = list(range(soon, pieces - direct))
    tail = list(range(pieces - direct, pieces))
    split = len(middle) - SOON_AT
    order = middle[:TAIL_AT] + tail + middle[TAIL_AT:split] + list(range(soon)) + middle[split:]
    ends = middle + list(range(soon)) + tail
    ready = [soon]
    for i in range(pieces):
        ready.append(ready[-1])
        while ready[-1] in order[:i + 1]:
            ready[-1] += 1

    def look(table, i):
        value = table[0] + i * (table[1] - table[0])
        for j in range(1, len(table) - 1):
            if table[j + 1] - table[j] != table[j] - table[j - 1] or j == len(table) - 2:
                value = jnp.where(i >= j, table[j] + (i - j) * (table[j + 1] - table[j]), value)
        return value

    def place_of(p):
        at = p - soon + jnp.where(p < soon, pieces, 0)
        return at // heads, at % heads

    def chained(i):
        return look(order, i)

    def slot(c):
        return handed + c * (1 - 2 * handed)

    barrier = pltpu.get_barrier_semaphore()

    @pl.when(s > 0)
    def _():
        pl.semaphore_signal(barrier, inc=1, device_id=(r, (s + n - 1) % n), device_id_type=MESH)

    @pl.when(s < n - 1)
    def _():
        pl.semaphore_signal(barrier, inc=1, device_id=(r, n - 1), device_id_type=MESH)

    pl.semaphore_signal(barrier, inc=1, device_id=(partner, s), device_id_type=MESH)
    loads = [
        pltpu.make_async_copy(src, dst, load_sem.at[i])
        for i, (src, dst) in enumerate(
            ((k_hbm, k_ref), (v_hbm, v_ref), (q_hbm, q_ref), (do_hbm, do_ref))
        )
    ]
    for load in loads:
        load.start()

    @pl.when(s == n - 1)
    def _():
        pl.semaphore_wait(barrier, n)
        for t in range(n - 2):
            pl.semaphore_signal(far, inc=1, device_id=(r, t), device_id_type=MESH)

    loads[0].wait()
    loads[1].wait()

    for c in range(2):
        epbuf[s, c:c + 1, 0:rows] = jnp.where(
            slot(c) == 0, ep_ref[0:1, :], ep_ref[1:2, :]
        )
        for g in range(heads):
            kvbuf[c, g, own, 0:DH] = k_ref[slot(c), :, g * DH:(g + 1) * DH]
            kvbuf[c, g, own, DH:2 * DH] = v_ref[slot(c), :, g * DH:(g + 1) * DH]

    @pl.when(s < n - 1)
    def _():
        pl.semaphore_wait(barrier, 2)

    def chunk(t, skip=0):
        return pl.ds(pl.multiple_of(t * rows + skip, 16), rows - skip)

    def up_own(p, t):
        part = kvbuf.at[(*place_of(p), chunk(t))]
        return pltpu.make_async_remote_copy(
            src_ref=part, dst_ref=part, send_sem=own_send, recv_sem=own_recv.at[p],
            device_id=(r, above), device_id_type=MESH,
        )

    def up_fwd(p, k):
        part = kvbuf.at[(*place_of(p), pl.ds(low(k), k * rows - low(k)))]
        return pltpu.make_async_remote_copy(
            src_ref=part, dst_ref=part, send_sem=fwd_send.at[place_of(p)[0]], recv_sem=fwd_recv.at[p],
            device_id=(r, above), device_id_type=MESH,
        )

    def up_far(p, t):
        part = kvbuf.at[(*place_of(p), chunk(t, first(n - 1 - t)))]
        return pltpu.make_async_remote_copy(
            src_ref=part, dst_ref=part, send_sem=far_send, recv_sem=far_recv.at[p, t],
            device_id=(r, n - 1), device_id_type=MESH,
        )

    def ep_far(t):
        return pltpu.make_async_remote_copy(
            src_ref=epbuf.at[t], dst_ref=epbuf.at[t],
            send_sem=ep_send.at[n - 1], recv_sem=ep_recv.at[t],
            device_id=(r, n - 1), device_id_type=MESH,
        )

    def ep_copy(t):
        return pltpu.make_async_remote_copy(
            src_ref=epbuf.at[t], dst_ref=epbuf.at[t],
            send_sem=ep_send.at[t], recv_sem=ep_recv.at[t],
            device_id=(r, above), device_id_type=MESH,
        )

    def down_sum(p):
        part = (*place_of(p), pl.ds(low(n - 2), top - low(n - 2)))
        return pltpu.make_async_remote_copy(
            src_ref=gpart.at[part], dst_ref=grecv.at[part],
            send_sem=acc_send.at[place_of(p)[0]], recv_sem=acc_recv.at[p],
            device_id=(r, (s + n - 1) % n), device_id_type=MESH,
        )

    def down(p, d):
        c, g = place_of(p)
        return pltpu.make_async_remote_copy(
            src_ref=gpart.at[c, g, chunk((s + n - d) % n, first(d))],
            dst_ref=grecv.at[c, g, chunk(s, first(d))],
            send_sem=down_send.at[d], recv_sem=down_recv.at[p, s],
            device_id=(r, (s + n - d) % n), device_id_type=MESH,
        )

    def down_arrival(p, d):
        c, g = place_of(p)
        part = grecv.at[c, g, chunk((s + d) % n, first(d))]
        return pltpu.make_async_remote_copy(
            src_ref=part, dst_ref=part,
            send_sem=down_send.at[d], recv_sem=down_recv.at[p, (s + d) % n],
            device_id=(r, (s + d) % n), device_id_type=MESH,
        )

    def send_down(p):
        for d in reversed(reach):
            @pl.when(s >= d)
            def _(d=d):
                down(p, d).start()

    def trade(which, g, buf, out, width):
        cols = pl.ds(pl.multiple_of(g * width, width), width)
        return pltpu.make_async_remote_copy(
            src_ref=buf.at[0, :, cols], dst_ref=out.at[1, :, cols],
            send_sem=trade_send.at[which], recv_sem=trade_recv.at[which],
            device_id=(partner, s), device_id_type=MESH,
        )

    def keep(which, g, buf, out, width):
        cols = pl.ds(pl.multiple_of(g * width, width), width)
        return pltpu.make_async_copy(
            buf.at[1, :, cols], out.at[0, :, cols], keep_sem.at[which]
        )

    lead = jnp.where(s == n - 2, LEAD_TOP, LEAD)

    @pl.when(s < n - 1)
    def _():
        ep_copy(s).start()

        def early(i, carry):
            up_own(jnp.where(s == n - 2, i, chained(i)), s).start()
            return carry

        lax.fori_loop(0, lead, early, 0)

    for t in range(n - 2):
        @pl.when(s == t)
        def _(t=t):
            pl.semaphore_wait(far, 1)
            ep_far(t).start()
            if n - 1 - t in reach:
                for p in range(soon):
                    up_far(p, t).start()

    @pl.when(s == 0)
    def _():
        def remaining(i, carry):
            up_own(chained(i), s).start()
            return carry

        lax.fori_loop(lead, pieces, remaining, 0)

    def clear(at, size):
        def one(i, carry):
            kvbuf[i // heads, i % heads, pl.ds(at, size), :] = (
                jnp.zeros((size, 2 * DH), jnp.bfloat16)
            )
            return carry

        lax.fori_loop(0, 2 * heads, one, 0)

    eye = lax.broadcasted_iota(jnp.int32, (rows, DH), 0) == lax.broadcasted_iota(
        jnp.int32, (rows, DH), 1
    )

    def see(t):
        def one(c, carry):
            mine = epbuf[s, pl.ds(c, 1), 0:rows]
            mine = jnp.concatenate([mine] * groups, axis=1)
            pos_q = jnp.concatenate(
                [s * rows + lax.broadcasted_iota(jnp.int32, (rows, rows), 1)] * groups, axis=1
            )
            line = epbuf[t, pl.ds(c, 1), :]
            column = jnp.sum(jnp.where(eye, line, 0), axis=1, keepdims=True)
            pos_k = t * rows + lax.broadcasted_iota(jnp.int32, (rows, wide), 0)
            seen = jnp.where(pos_k <= pos_q, 1.0, 0.0) * jnp.where(column == mine, 1.0, 0.0)
            allow[c, chunk(t), :] = seen
            return carry

        lax.fori_loop(0, 2, one, 0)

    for t in range(n):
        @pl.when(t > s)
        def _(t=t):
            clear(t * rows, rows)
            for c in range(2):
                allow[c, t * rows:(t + 1) * rows, :] = jnp.zeros((rows, wide), jnp.float32)
    for k in range(1, n):
        if low(k - 1) > 0:
            @pl.when(s == k)
            def _(k=k):
                clear(0, low(k - 1))
    see(s)
    loads[2].wait()
    loads[3].wait()

    def ep_step(d, carry):
        t = s - d
        ep_copy(t).wait_recv()

        @pl.when(s < n - 2)
        def _():
            ep_copy(t).start()
        see(t)
        return carry

    lax.fori_loop(1, s + 1, ep_step, 0)

    def forward(i):
        p = jnp.where(s == n - 1, i, chained(i))

        @pl.when(s > 0)
        def _():
            up_own(p, (s + n - 1) % n).wait_recv()
        for k in range(1, n):
            @pl.when(s == k)
            def _(k=k):
                if k == n - 1:
                    @pl.when(p < soon)
                    def _():
                        for t in range(n - 2):
                            if n - 1 - t in reach:
                                up_far(p, t).wait_recv()

                    @pl.when(p >= soon)
                    def _():
                        up_fwd(p, k - 1).wait_recv()
                elif k == n - 2:
                    up_fwd(p, k - 1).wait_recv()
                    was, now = look(ready, i), look(ready, i + 1)

                    def pass_on(f, carry):
                        @pl.when(f + lead - soon < pieces)
                        def _():
                            up_own(f + lead - soon, s).start()
                        up_fwd(f, k).start()
                        return carry

                    lax.fori_loop(was, now, pass_on, 0)
                else:
                    if k > 1:
                        up_fwd(p, k - 1).wait_recv()
                    up_fwd(p, k).start()

    def compute(p):
        c, g = place_of(p)
        at = slot(c)

        def stack(ref):
            return jnp.concatenate(
                [
                    ref[at, :, pl.ds(pl.multiple_of((g * groups + i) * DH, DH), DH)]
                    for i in range(groups)
                ],
                axis=0,
            )

        q = stack(q_ref)
        do = stack(do_ref)
        key = kvbuf[c, g, :, 0:DH]
        value = kvbuf[c, g, :, DH:2 * DH]
        scores = jnp.where(allow[c] > 0.5, dot(key, q, NT) * scaling, jnp.float32(-1e30))
        peak = jnp.max(scores, axis=0, keepdims=True)
        expo = jnp.exp(scores - peak)
        probs = expo * (1.0 / jnp.sum(expo, axis=0, keepdims=True))
        dprobs = dot(value, do, NT)
        delta = jnp.sum(probs * dprobs, axis=0, keepdims=True)
        dscores = (probs * (dprobs - delta)).astype(jnp.bfloat16)
        gk = dot(dscores, q, NN)
        gv = dot(probs.astype(jnp.bfloat16), do, NN)
        gown[c, g, :, 0:DH] = gk
        gown[c, g, :, DH:2 * DH] = gv
        gpart[c, g, :, 0:DH] = gk.astype(jnp.bfloat16)
        gpart[c, g, :, DH:2 * DH] = gv.astype(jnp.bfloat16)

        @pl.when((s == n - 1) & summed(p))
        def _():
            down_sum(p).start()

        @pl.when((s < n - 2) | jnp.logical_not(summed(p)))
        def _():
            send_down(p)

        gq = (dot(dscores, key, TN) * scaling).astype(jnp.bfloat16)
        for i in range(groups):
            cols = pl.ds(pl.multiple_of((g * groups + i) * DH, DH), DH)
            tq[c, :, cols] = gq[i * rows:(i + 1) * rows]

        @pl.when(c == 0)
        def _():
            trade(0, g, tq, gq_out, groups * DH).start()

        @pl.when(c == 1)
        def _():
            keep(0, g, tq, gq_out, groups * DH).start()

    def finish(p):
        c, g = place_of(p)

        @pl.when((s == n - 2) & summed(p))
        def _():
            part = (c, g, pl.ds(low(n - 2), top - low(n - 2)))
            down_sum(p).wait_recv()
            total = gown[part] + grecv[part].astype(jnp.float32)
            gown[part] = total
            gpart[part] = total.astype(jnp.bfloat16)
            send_down(p)

        for d in reach:
            @pl.when((s + d < n - 1) | ((s + d == n - 1) & jnp.logical_not(summed(p))))
            def _(d=d):
                down_arrival(p, d).wait_recv()
                part = (c, g, chunk(s, first(d)))
                gown[part] += grecv[c, g, chunk(s + d, first(d))].astype(jnp.float32)

        cols = pl.ds(pl.multiple_of(g * DH, DH), DH)
        tk[c, :, cols] = (gown[c, g, own, 0:DH] * scaling).astype(jnp.bfloat16)
        tv[c, :, cols] = gown[c, g, own, DH:2 * DH].astype(jnp.bfloat16)

        @pl.when(c == 0)
        def _():
            trade(1, g, tk, gk_out, DH).start()
            trade(2, g, tv, gv_out, DH).start()

        @pl.when(c == 1)
        def _():
            keep(1, g, tk, gk_out, DH).start()
            keep(2, g, tv, gv_out, DH).start()

    back = jnp.where((s == 0) | (s == n - 1), 0, jnp.where(s == n - 2, BACK_TOP, BACK))
    late = back + jnp.where(s == n - 1, 0, jnp.where(s == n - 2, LAG, pieces))

    def step(i, carry):
        @pl.when((s > 0) & (s < n - 2) & (i + lead < pieces))
        def _():
            up_own(chained(i + lead), s).start()

        @pl.when(i < pieces)
        def _():
            forward(i)

        @pl.when((i >= back) & (i < pieces + back))
        def _():
            compute(jnp.where(s == n - 1, i, chained(i - back)))

        @pl.when(i >= late)
        def _():
            finish(jnp.where(s == n - 1, i, look(ends, i - late)))
        return carry

    lax.fori_loop(0, pieces + late, step, 0)

    def sent(part, sem):
        pltpu.make_async_remote_copy(
            src_ref=part, dst_ref=part, send_sem=sem, recv_sem=sem,
            device_id=(r, above), device_id_type=MESH,
        ).wait_send()

    @pl.when(s < n - 1)
    def _():
        sent(kvbuf.at[:, :, own, :], own_send)

        def one(t, carry):
            ep_copy(t).wait_send()
            return carry

        lax.fori_loop(jnp.where(s == n - 2, s, 0), s + 1, one, 0)

    for t in range(n - 2):
        @pl.when(s == t)
        def _(t=t):
            ep_far(t).wait_send()
            if n - 1 - t in reach:
                sent(kvbuf.at[1, heads - soon:heads, chunk(t, first(n - 1 - t)), :], far_send)

    for k in range(1, n - 1):
        @pl.when(s == k)
        def _(k=k):
            held = pl.ds(low(k), k * rows - low(k))
            sent(kvbuf.at[0, :, held, :], fwd_send.at[0])
            sent(kvbuf.at[1, 0:heads - (soon if k == n - 2 else 0), held, :], fwd_send.at[1])

    for d in reach:
        @pl.when((s >= d) & (s < n - 1))
        def _(d=d):
            sent(gpart.at[:, :, chunk(s - d, first(d))], down_send.at[d])

    @pl.when(s == n - 1)
    def _():
        rest = pl.ds(low(n - 2), top - low(n - 2))
        sent(gpart.at[0, :, rest], acc_send.at[0])
        sent(gpart.at[1, 0:heads - direct - soon, rest], acc_send.at[1])
        for d in reach:
            sent(gpart.at[0, 0:soon + direct, chunk(s - d, first(d))], down_send.at[d])

    for which, buf, out in ((0, tq, gq_out), (1, tk, gk_out), (2, tv, gv_out)):
        pltpu.make_async_remote_copy(
            src_ref=buf.at[0], dst_ref=out.at[1],
            send_sem=trade_send.at[which], recv_sem=trade_recv.at[which],
            device_id=(partner, s), device_id_type=MESH,
        ).wait()
        pltpu.make_async_copy(buf.at[1], out.at[0], keep_sem.at[which]).wait()


def call(n, ndp, mask, send_slot, episodes, queries, key_rows, value_rows, cotangent):
    rows = queries.shape[1]
    heads = key_rows.shape[2] // DH
    groups = queries.shape[2] // key_rows.shape[2]
    pieces = 2 * heads
    vmem = pl.BlockSpec(memory_space=pltpu.VMEM)
    dma = pltpu.SemaphoreType.DMA
    return pl.pallas_call(
        functools.partial(kernel, n, ndp, mask),
        out_shape=[
            jax.ShapeDtypeStruct(x.shape, x.dtype) for x in (queries, key_rows, value_rows)
        ],
        in_specs=[pl.BlockSpec(memory_space=pltpu.SMEM), vmem]
        + [pl.BlockSpec(memory_space=pl.ANY)] * 4,
        out_specs=[pl.BlockSpec(memory_space=pl.ANY)] * 3,
        scratch_shapes=[
            pltpu.VMEM(queries.shape, jnp.bfloat16),
            pltpu.VMEM(key_rows.shape, jnp.bfloat16),
            pltpu.VMEM(value_rows.shape, jnp.bfloat16),
            pltpu.VMEM(cotangent.shape, jnp.bfloat16),
            dma((4,)),
            dma((3,)),
            pltpu.VMEM((2, heads, n * rows, 2 * DH), jnp.bfloat16),
            pltpu.VMEM((n, 8, DH), jnp.int32),
            pltpu.VMEM((2, n * rows, groups * rows), jnp.float32),
            pltpu.VMEM((2, heads, n * rows, 2 * DH), jnp.bfloat16),
            pltpu.VMEM((2, heads, n * rows, 2 * DH), jnp.float32),
            pltpu.VMEM((2, heads, n * rows, 2 * DH), jnp.bfloat16),
            pltpu.VMEM(queries.shape, jnp.bfloat16),
            pltpu.VMEM(key_rows.shape, jnp.bfloat16),
            pltpu.VMEM(value_rows.shape, jnp.bfloat16),
            pltpu.SemaphoreType.REGULAR,
            dma,
            dma((max(1, min(SOON, heads)), n)),
            dma,
            dma((pieces,)),
            dma((2,)),
            dma((pieces,)),
            dma((n,)),
            dma((n,)),
            dma((2,)),
            dma((pieces,)),
            dma((n,)),
            dma((pieces, n)),
            dma((3,)),
            dma((3,)),
        ],
        compiler_params=pltpu.CompilerParams(
            collective_id=mask, has_side_effects=True, vmem_limit_bytes=48 << 20
        ),
    )(send_slot, episodes, queries, key_rows, value_rows, cotangent)


def settle(*refs):
    half = len(refs) // 2
    copies = [
        pltpu.make_async_copy(src, dst, refs[-1].at[i])
        for i, (src, dst) in enumerate(zip(refs[:half], refs[half:-1]))
    ]
    for copy in copies:
        copy.start()
    for copy in copies:
        copy.wait()


def place(*grads):
    anywhere = pl.BlockSpec(memory_space=pl.ANY)
    return pl.pallas_call(
        settle,
        out_shape=[jax.ShapeDtypeStruct(x.shape, x.dtype) for x in grads],
        in_specs=[anywhere] * len(grads),
        out_specs=[anywhere] * len(grads),
        scratch_shapes=[pltpu.SemaphoreType.DMA((len(grads),))],
    )(*grads)


def solution(mesh):
    n, ndp = mesh.shape["seq"], mesh.shape["dp"]

    def per_device(queries, key_rows, value_rows, cotangent, episodes, send_slot, swap_mask):
        grads = lax.switch(
            swap_mask[0] - 1,
            [functools.partial(call, n, ndp, mask) for mask in range(1, ndp)],
            send_slot, episodes, queries, key_rows, value_rows, cotangent,
        )
        return tuple(place(*grads))

    in_specs = (
        P("dp", "seq", None),
        P("dp", "seq", None),
        P("dp", "seq", None),
        P("dp", "seq", None),
        P("dp", "seq"),
        P("dp"),
        P(),
    )
    out_specs = (P("dp", "seq", None), P("dp", "seq", None), P("dp", "seq", None))
    return jax.shard_map(
        per_device, mesh=mesh, in_specs=in_specs, out_specs=out_specs, check_vma=False
    )
```

```python
import functools

import jax
import jax.numpy as jnp
from jax import lax
from jax.experimental import pallas as pl
from jax.experimental.pallas import tpu as pltpu
from jax.sharding import PartitionSpec as P

DH = 128
LEAD_TOP = 5
LEAD = 3
LAG = 5
BACK = 6
BACK_TOP = 1
DIRECT = 1
SOON = 2
TAIL_AT = 6
SOON_AT = 1
MESH = pl.DeviceIdType.MESH
NT = (((1,), (1,)), ((), ()))
NN = (((1,), (0,)), ((), ()))
TN = (((0,), (0,)), ((), ()))


def dot(a, b, dims):
    return lax.dot_general(a, b, dims, preferred_element_type=jnp.float32)


def kernel(
    n, ndp, mask, send_ref, ep_ref, q_hbm, k_hbm, v_hbm, do_hbm,
    gq_out, gk_out, gv_out,
    q_ref, k_ref, v_ref, do_ref, load_sem, keep_sem, kvbuf, epbuf, allow, gpart, gown, grecv, tq, tk, tv,
    far, far_send, far_recv, own_send, own_recv, fwd_send, fwd_recv, ep_send, ep_recv, acc_send, acc_recv, down_send, down_recv,
    trade_send, trade_recv,
):
    r = lax.axis_index("dp")
    s = lax.axis_index("seq")
    rows = q_ref.shape[1]
    heads = k_ref.shape[2] // DH
    groups = q_ref.shape[2] // k_ref.shape[2]
    pieces = 2 * heads
    direct = min(DIRECT, heads)
    soon = min(SOON, heads)
    wide = groups * rows
    scaling = 1.0 / jnp.sqrt(jnp.float32(DH))
    partner = r
    for b in range(ndp.bit_length() - 1):
        if (mask >> b) & 1:
            partner = partner + (1 << b) * (1 - 2 * ((r // (1 << b)) % 2))
    handed = send_ref[0]
    most = 2 * n * rows // 3

    def first(d):
        return min(max(0, d * rows - most + 1) // 16 * 16, rows)

    def low(k):
        return max(0, (k + 1) * rows - most + 1) // 16 * 16

    reach = [d for d in range(1, n) if first(d) < rows]
    own = pl.ds(pl.multiple_of(s * rows, rows), rows)
    top = (n - 2) * rows
    above = (s + 1) % n

    def summed(p):
        return (p >= soon) & (p < pieces - direct)

    middle = list(range(soon, pieces - direct))
    tail = list(range(pieces - direct, pieces))
    split = len(middle) - SOON_AT
    order = middle[:TAIL_AT] + tail + middle[TAIL_AT:split] + list(range(soon)) + middle[split:]
    ends = middle + list(range(soon)) + tail
    ready = [soon]
    for i in range(pieces):
        ready.append(ready[-1])
        while ready[-1] in order[:i + 1]:
            ready[-1] += 1

    def look(table, i):
        value = table[0] + i * (table[1] - table[0])
        for j in range(1, len(table) - 1):
            if table[j + 1] - table[j] != table[j] - table[j - 1] or j == len(table) - 2:
                value = jnp.where(i >= j, table[j] + (i - j) * (table[j + 1] - table[j]), value)
        return value

    def place_of(p):
        at = p - soon + jnp.where(p < soon, pieces, 0)
        return at // heads, at % heads

    def chained(i):
        return look(order, i)

    def slot(c):
        return handed + c * (1 - 2 * handed)

    barrier = pltpu.get_barrier_semaphore()

    @pl.when(s > 0)
    def _():
        pl.semaphore_signal(barrier, inc=1, device_id=(r, (s + n - 1) % n), device_id_type=MESH)

    @pl.when(s < n - 1)
    def _():
        pl.semaphore_signal(barrier, inc=1, device_id=(r, n - 1), device_id_type=MESH)

    pl.semaphore_signal(barrier, inc=1, device_id=(partner, s), device_id_type=MESH)
    loads = [
        pltpu.make_async_copy(src, dst, load_sem.at[i])
        for i, (src, dst) in enumerate(
            ((k_hbm, k_ref), (v_hbm, v_ref), (q_hbm, q_ref), (do_hbm, do_ref))
        )
    ]
    for load in loads:
        load.start()

    @pl.when(s == n - 1)
    def _():
        pl.semaphore_wait(barrier, n)
        for t in range(n - 2):
            pl.semaphore_signal(far, inc=1, device_id=(r, t), device_id_type=MESH)

    loads[0].wait()
    loads[1].wait()

    for c in range(2):
        epbuf[s, c:c + 1, 0:rows] = jnp.where(
            slot(c) == 0, ep_ref[0:1, :], ep_ref[1:2, :]
        )
        for g in range(heads):
            kvbuf[c, g, own, 0:DH] = k_ref[slot(c), :, g * DH:(g + 1) * DH]
            kvbuf[c, g, own, DH:2 * DH] = v_ref[slot(c), :, g * DH:(g + 1) * DH]

    @pl.when(s < n - 1)
    def _():
        pl.semaphore_wait(barrier, 2)

    def chunk(t, skip=0):
        return pl.ds(pl.multiple_of(t * rows + skip, 16), rows - skip)

    def up_own(p, t):
        part = kvbuf.at[(*place_of(p), chunk(t))]
        return pltpu.make_async_remote_copy(
            src_ref=part, dst_ref=part, send_sem=own_send, recv_sem=own_recv.at[p],
            device_id=(r, above), device_id_type=MESH,
        )

    def up_fwd(p, k):
        part = kvbuf.at[(*place_of(p), pl.ds(low(k), k * rows - low(k)))]
        return pltpu.make_async_remote_copy(
            src_ref=part, dst_ref=part, send_sem=fwd_send.at[place_of(p)[0]], recv_sem=fwd_recv.at[p],
            device_id=(r, above), device_id_type=MESH,
        )

    def up_far(p, t):
        part = kvbuf.at[(*place_of(p), chunk(t, first(n - 1 - t)))]
        return pltpu.make_async_remote_copy(
            src_ref=part, dst_ref=part, send_sem=far_send, recv_sem=far_recv.at[p, t],
            device_id=(r, n - 1), device_id_type=MESH,
        )

    def ep_far(t):
        return pltpu.make_async_remote_copy(
            src_ref=epbuf.at[t], dst_ref=epbuf.at[t],
            send_sem=ep_send.at[n - 1], recv_sem=ep_recv.at[t],
            device_id=(r, n - 1), device_id_type=MESH,
        )

    def ep_copy(t):
        return pltpu.make_async_remote_copy(
            src_ref=epbuf.at[t], dst_ref=epbuf.at[t],
            send_sem=ep_send.at[t], recv_sem=ep_recv.at[t],
            device_id=(r, above), device_id_type=MESH,
        )

    def down_sum(p):
        part = (*place_of(p), pl.ds(low(n - 2), top - low(n - 2)))
        return pltpu.make_async_remote_copy(
            src_ref=gpart.at[part], dst_ref=grecv.at[part],
            send_sem=acc_send.at[place_of(p)[0]], recv_sem=acc_recv.at[p],
            device_id=(r, (s + n - 1) % n), device_id_type=MESH,
        )

    def down(p, d):
        c, g = place_of(p)
        return pltpu.make_async_remote_copy(
            src_ref=gpart.at[c, g, chunk((s + n - d) % n, first(d))],
            dst_ref=grecv.at[c, g, chunk(s, first(d))],
            send_sem=down_send.at[d], recv_sem=down_recv.at[p, s],
            device_id=(r, (s + n - d) % n), device_id_type=MESH,
        )

    def down_arrival(p, d):
        c, g = place_of(p)
        part = grecv.at[c, g, chunk((s + d) % n, first(d))]
        return pltpu.make_async_remote_copy(
            src_ref=part, dst_ref=part,
            send_sem=down_send.at[d], recv_sem=down_recv.at[p, (s + d) % n],
            device_id=(r, (s + d) % n), device_id_type=MESH,
        )

    def send_down(p):
        for d in reversed(reach):
            @pl.when(s >= d)
            def _(d=d):
                down(p, d).start()

    def trade(which, g, buf, out, width):
        cols = pl.ds(pl.multiple_of(g * width, width), width)
        return pltpu.make_async_remote_copy(
            src_ref=buf.at[0, :, cols], dst_ref=out.at[1, :, cols],
            send_sem=trade_send.at[which], recv_sem=trade_recv.at[which],
            device_id=(partner, s), device_id_type=MESH,
        )

    def keep(which, g, buf, out, width):
        cols = pl.ds(pl.multiple_of(g * width, width), width)
        return pltpu.make_async_copy(
            buf.at[1, :, cols], out.at[0, :, cols], keep_sem.at[which]
        )

    lead = jnp.where(s == n - 2, LEAD_TOP, LEAD)

    @pl.when(s < n - 1)
    def _():
        ep_copy(s).start()

        def early(i, carry):
            up_own(jnp.where(s == n - 2, i, chained(i)), s).start()
            return carry

        lax.fori_loop(0, lead, early, 0)

    for t in range(n - 2):
        @pl.when(s == t)
        def _(t=t):
            pl.semaphore_wait(far, 1)
            ep_far(t).start()
            if n - 1 - t in reach:
                for p in range(soon):
                    up_far(p, t).start()

    @pl.when(s == 0)
    def _():
        def remaining(i, carry):
            up_own(chained(i), s).start()
            return carry

        lax.fori_loop(lead, pieces, remaining, 0)

    def clear(at, size):
        def one(i, carry):
            kvbuf[i // heads, i % heads, pl.ds(at, size), :] = (
                jnp.zeros((size, 2 * DH), jnp.bfloat16)
            )
            return carry

        lax.fori_loop(0, 2 * heads, one, 0)

    eye = lax.broadcasted_iota(jnp.int32, (rows, DH), 0) == lax.broadcasted_iota(
        jnp.int32, (rows, DH), 1
    )

    def see(t):
        def one(c, carry):
            mine = epbuf[s, pl.ds(c, 1), 0:rows]
            mine = jnp.concatenate([mine] * groups, axis=1)
            pos_q = jnp.concatenate(
                [s * rows + lax.broadcasted_iota(jnp.int32, (rows, rows), 1)] * groups, axis=1
            )
            line = epbuf[t, pl.ds(c, 1), :]
            column = jnp.sum(jnp.where(eye, line, 0), axis=1, keepdims=True)
            pos_k = t * rows + lax.broadcasted_iota(jnp.int32, (rows, wide), 0)
            seen = jnp.where(pos_k <= pos_q, 1.0, 0.0) * jnp.where(column == mine, 1.0, 0.0)
            allow[c, chunk(t), :] = seen
            return carry

        lax.fori_loop(0, 2, one, 0)

    for t in range(n):
        @pl.when(t > s)
        def _(t=t):
            clear(t * rows, rows)
            for c in range(2):
                allow[c, t * rows:(t + 1) * rows, :] = jnp.zeros((rows, wide), jnp.float32)
    for k in range(1, n):
        if low(k - 1) > 0:
            @pl.when(s == k)
            def _(k=k):
                clear(0, low(k - 1))
    see(s)
    loads[2].wait()
    loads[3].wait()

    def ep_step(d, carry):
        t = s - d
        ep_copy(t).wait_recv()

        @pl.when(s < n - 2)
        def _():
            ep_copy(t).start()
        see(t)
        return carry

    lax.fori_loop(1, s + 1, ep_step, 0)

    def forward(i):
        p = jnp.where(s == n - 1, i, chained(i))

        @pl.when(s > 0)
        def _():
            up_own(p, (s + n - 1) % n).wait_recv()
        for k in range(1, n):
            @pl.when(s == k)
            def _(k=k):
                if k == n - 1:
                    @pl.when(p < soon)
                    def _():
                        for t in range(n - 2):
                            if n - 1 - t in reach:
                                up_far(p, t).wait_recv()

                    @pl.when(p >= soon)
                    def _():
                        up_fwd(p, k - 1).wait_recv()
                elif k == n - 2:
                    up_fwd(p, k - 1).wait_recv()
                    was, now = look(ready, i), look(ready, i + 1)

                    def pass_on(f, carry):
                        @pl.when(f + lead - soon < pieces)
                        def _():
                            up_own(f + lead - soon, s).start()
                        up_fwd(f, k).start()
                        return carry

                    lax.fori_loop(was, now, pass_on, 0)
                else:
                    if k > 1:
                        up_fwd(p, k - 1).wait_recv()
                    up_fwd(p, k).start()

    def compute(p):
        c, g = place_of(p)
        at = slot(c)

        def stack(ref):
            return jnp.concatenate(
                [
                    ref[at, :, pl.ds(pl.multiple_of((g * groups + i) * DH, DH), DH)]
                    for i in range(groups)
                ],
                axis=0,
            )

        q = stack(q_ref)
        do = stack(do_ref)
        key = kvbuf[c, g, :, 0:DH]
        value = kvbuf[c, g, :, DH:2 * DH]
        scores = jnp.where(allow[c] > 0.5, dot(key, q, NT) * scaling, jnp.float32(-1e30))
        peak = jnp.max(scores, axis=0, keepdims=True)
        expo = jnp.exp(scores - peak)
        probs = expo * (1.0 / jnp.sum(expo, axis=0, keepdims=True))
        dprobs = dot(value, do, NT)
        delta = jnp.sum(probs * dprobs, axis=0, keepdims=True)
        dscores = (probs * (dprobs - delta)).astype(jnp.bfloat16)
        gk = dot(dscores, q, NN)
        gv = dot(probs.astype(jnp.bfloat16), do, NN)
        gown[c, g, :, 0:DH] = gk
        gown[c, g, :, DH:2 * DH] = gv
        gpart[c, g, :, 0:DH] = gk.astype(jnp.bfloat16)
        gpart[c, g, :, DH:2 * DH] = gv.astype(jnp.bfloat16)

        @pl.when((s == n - 1) & summed(p))
        def _():
            down_sum(p).start()
            down(p, 1).start()

        @pl.when((s < n - 2) | jnp.logical_not(summed(p)))
        def _():
            send_down(p)

        gq = (dot(dscores, key, TN) * scaling).astype(jnp.bfloat16)
        for i in range(groups):
            cols = pl.ds(pl.multiple_of((g * groups + i) * DH, DH), DH)
            tq[c, :, cols] = gq[i * rows:(i + 1) * rows]

        @pl.when(c == 0)
        def _():
            trade(0, g, tq, gq_out, groups * DH).start()

        @pl.when(c == 1)
        def _():
            keep(0, g, tq, gq_out, groups * DH).start()

    def finish(p):
        c, g = place_of(p)

        @pl.when((s == n - 2) & summed(p))
        def _():
            part = (c, g, pl.ds(low(n - 2), top - low(n - 2)))
            down_sum(p).wait_recv()
            total = gown[part] + grecv[part].astype(jnp.float32)
            gown[part] = total
            gpart[part] = total.astype(jnp.bfloat16)
            send_down(p)

        for d in reach:
            @pl.when((s + d < n - 1) | ((s + d == n - 1) & (jnp.logical_not(summed(p)) | (d == 1))))
            def _(d=d):
                down_arrival(p, d).wait_recv()
                part = (c, g, chunk(s, first(d)))
                gown[part] += grecv[c, g, chunk(s + d, first(d))].astype(jnp.float32)

        cols = pl.ds(pl.multiple_of(g * DH, DH), DH)
        tk[c, :, cols] = (gown[c, g, own, 0:DH] * scaling).astype(jnp.bfloat16)
        tv[c, :, cols] = gown[c, g, own, DH:2 * DH].astype(jnp.bfloat16)

        @pl.when(c == 0)
        def _():
            trade(1, g, tk, gk_out, DH).start()
            trade(2, g, tv, gv_out, DH).start()

        @pl.when(c == 1)
        def _():
            keep(1, g, tk, gk_out, DH).start()
            keep(2, g, tv, gv_out, DH).start()

    back = jnp.where((s == 0) | (s == n - 1), 0, jnp.where(s == n - 2, BACK_TOP, BACK))
    late = back + jnp.where(s == n - 1, 0, jnp.where(s == n - 2, LAG, pieces))

    def step(i, carry):
        @pl.when((s > 0) & (s < n - 2) & (i + lead < pieces))
        def _():
            up_own(chained(i + lead), s).start()

        @pl.when(i < pieces)
        def _():
            forward(i)

        @pl.when((i >= back) & (i < pieces + back))
        def _():
            compute(jnp.where(s == n - 1, i, chained(i - back)))

        @pl.when(i >= late)
        def _():
            finish(jnp.where(s == n - 1, i, look(ends, i - late)))
        return carry

    lax.fori_loop(0, pieces + late, step, 0)

    def sent(part, sem):
        pltpu.make_async_remote_copy(
            src_ref=part, dst_ref=part, send_sem=sem, recv_sem=sem,
            device_id=(r, above), device_id_type=MESH,
        ).wait_send()

    @pl.when(s < n - 1)
    def _():
        sent(kvbuf.at[:, :, own, :], own_send)

        def one(t, carry):
            ep_copy(t).wait_send()
            return carry

        lax.fori_loop(jnp.where(s == n - 2, s, 0), s + 1, one, 0)

    for t in range(n - 2):
        @pl.when(s == t)
        def _(t=t):
            ep_far(t).wait_send()
            if n - 1 - t in reach:
                sent(kvbuf.at[1, heads - soon:heads, chunk(t, first(n - 1 - t)), :], far_send)

    for k in range(1, n - 1):
        @pl.when(s == k)
        def _(k=k):
            held = pl.ds(low(k), k * rows - low(k))
            sent(kvbuf.at[0, :, held, :], fwd_send.at[0])
            sent(kvbuf.at[1, 0:heads - (soon if k == n - 2 else 0), held, :], fwd_send.at[1])

    for d in reach:
        @pl.when((s >= d) & (s < n - 1))
        def _(d=d):
            sent(gpart.at[:, :, chunk(s - d, first(d))], down_send.at[d])

    @pl.when(s == n - 1)
    def _():
        rest = pl.ds(low(n - 2), top - low(n - 2))
        sent(gpart.at[0, :, rest], acc_send.at[0])
        sent(gpart.at[1, 0:heads - direct - soon, rest], acc_send.at[1])
        for d in reach:
            if d == 1:
                sent(gpart.at[:, :, chunk(s - d, first(d))], down_send.at[d])
            else:
                sent(gpart.at[0, 0:soon + direct, chunk(s - d, first(d))], down_send.at[d])

    for which, buf, out in ((0, tq, gq_out), (1, tk, gk_out), (2, tv, gv_out)):
        pltpu.make_async_remote_copy(
            src_ref=buf.at[0], dst_ref=out.at[1],
            send_sem=trade_send.at[which], recv_sem=trade_recv.at[which],
            device_id=(partner, s), device_id_type=MESH,
        ).wait()
        pltpu.make_async_copy(buf.at[1], out.at[0], keep_sem.at[which]).wait()


def call(n, ndp, mask, send_slot, episodes, queries, key_rows, value_rows, cotangent):
    rows = queries.shape[1]
    heads = key_rows.shape[2] // DH
    groups = queries.shape[2] // key_rows.shape[2]
    pieces = 2 * heads
    vmem = pl.BlockSpec(memory_space=pltpu.VMEM)
    dma = pltpu.SemaphoreType.DMA
    return pl.pallas_call(
        functools.partial(kernel, n, ndp, mask),
        out_shape=[
            jax.ShapeDtypeStruct(x.shape, x.dtype) for x in (queries, key_rows, value_rows)
        ],
        in_specs=[pl.BlockSpec(memory_space=pltpu.SMEM), vmem]
        + [pl.BlockSpec(memory_space=pl.ANY)] * 4,
        out_specs=[pl.BlockSpec(memory_space=pl.ANY)] * 3,
        scratch_shapes=[
            pltpu.VMEM(queries.shape, jnp.bfloat16),
            pltpu.VMEM(key_rows.shape, jnp.bfloat16),
            pltpu.VMEM(value_rows.shape, jnp.bfloat16),
            pltpu.VMEM(cotangent.shape, jnp.bfloat16),
            dma((4,)),
            dma((3,)),
            pltpu.VMEM((2, heads, n * rows, 2 * DH), jnp.bfloat16),
            pltpu.VMEM((n, 8, DH), jnp.int32),
            pltpu.VMEM((2, n * rows, groups * rows), jnp.float32),
            pltpu.VMEM((2, heads, n * rows, 2 * DH), jnp.bfloat16),
            pltpu.VMEM((2, heads, n * rows, 2 * DH), jnp.float32),
            pltpu.VMEM((2, heads, n * rows, 2 * DH), jnp.bfloat16),
            pltpu.VMEM(queries.shape, jnp.bfloat16),
            pltpu.VMEM(key_rows.shape, jnp.bfloat16),
            pltpu.VMEM(value_rows.shape, jnp.bfloat16),
            pltpu.SemaphoreType.REGULAR,
            dma,
            dma((max(1, min(SOON, heads)), n)),
            dma,
            dma((pieces,)),
            dma((2,)),
            dma((pieces,)),
            dma((n,)),
            dma((n,)),
            dma((2,)),
            dma((pieces,)),
            dma((n,)),
            dma((pieces, n)),
            dma((3,)),
            dma((3,)),
        ],
        compiler_params=pltpu.CompilerParams(
            collective_id=mask, has_side_effects=True, vmem_limit_bytes=48 << 20
        ),
    )(send_slot, episodes, queries, key_rows, value_rows, cotangent)


def settle(*refs):
    half = len(refs) // 2
    copies = [
        pltpu.make_async_copy(src, dst, refs[-1].at[i])
        for i, (src, dst) in enumerate(zip(refs[:half], refs[half:-1]))
    ]
    for copy in copies:
        copy.start()
    for copy in copies:
        copy.wait()


def place(*grads):
    anywhere = pl.BlockSpec(memory_space=pl.ANY)
    return pl.pallas_call(
        settle,
        out_shape=[jax.ShapeDtypeStruct(x.shape, x.dtype) for x in grads],
        in_specs=[anywhere] * len(grads),
        out_specs=[anywhere] * len(grads),
        scratch_shapes=[pltpu.SemaphoreType.DMA((len(grads),))],
    )(*grads)


def solution(mesh):
    n, ndp = mesh.shape["seq"], mesh.shape["dp"]

    def per_device(queries, key_rows, value_rows, cotangent, episodes, send_slot, swap_mask):
        grads = lax.switch(
            swap_mask[0] - 1,
            [functools.partial(call, n, ndp, mask) for mask in range(1, ndp)],
            send_slot, episodes, queries, key_rows, value_rows, cotangent,
        )
        return tuple(place(*grads))

    in_specs = (
        P("dp", "seq", None),
        P("dp", "seq", None),
        P("dp", "seq", None),
        P("dp", "seq", None),
        P("dp", "seq"),
        P("dp"),
        P(),
    )
    out_specs = (P("dp", "seq", None), P("dp", "seq", None), P("dp", "seq", None))
    return jax.shard_map(
        per_device, mesh=mesh, in_specs=in_specs, out_specs=out_specs, check_vma=False
    )
```

```python
import functools

import jax
import jax.numpy as jnp
from jax import lax
from jax.experimental import pallas as pl
from jax.experimental.pallas import tpu as pltpu
from jax.sharding import PartitionSpec as P

DH = 128
LEAD_TOP = 5
LEAD = 3
LAG = 5
BACK = 6
BACK_TOP = 1
DIRECT = 1
SOON = 2
TAIL_AT = 6
SOON_AT = 1
MESH = pl.DeviceIdType.MESH
NT = (((1,), (1,)), ((), ()))
NN = (((1,), (0,)), ((), ()))
TN = (((0,), (0,)), ((), ()))


def dot(a, b, dims):
    return lax.dot_general(a, b, dims, preferred_element_type=jnp.float32)


def kernel(
    n, ndp, mask, send_ref, ep_ref, q_hbm, k_hbm, v_hbm, do_hbm,
    gq_out, gk_out, gv_out,
    q_ref, k_ref, v_ref, do_ref, load_sem, keep_sem, kvbuf, epbuf, allow, gpart, gown, grecv, tq, tk, tv,
    far, far_send, far_recv, own_send, own_recv, fwd_send, fwd_recv, ep_send, ep_recv, acc_send, acc_recv, down_send, down_recv,
    trade_send, trade_recv,
):
    r = lax.axis_index("dp")
    s = lax.axis_index("seq")
    rows = q_ref.shape[1]
    heads = k_ref.shape[2] // DH
    groups = q_ref.shape[2] // k_ref.shape[2]
    pieces = 2 * heads
    direct = min(DIRECT, heads)
    soon = min(SOON, heads)
    wide = groups * rows
    scaling = 1.0 / jnp.sqrt(jnp.float32(DH))
    partner = r
    for b in range(ndp.bit_length() - 1):
        if (mask >> b) & 1:
            partner = partner + (1 << b) * (1 - 2 * ((r // (1 << b)) % 2))
    handed = send_ref[0]
    most = 2 * n * rows // 3

    def first(d):
        return min(max(0, d * rows - most + 1) // 16 * 16, rows)

    def low(k):
        return max(0, (k + 1) * rows - most + 1) // 16 * 16

    reach = [d for d in range(1, n) if first(d) < rows]
    own = pl.ds(pl.multiple_of(s * rows, rows), rows)
    top = (n - 2) * rows
    above = (s + 1) % n

    def summed(p):
        return (p >= soon) & (p < pieces - direct)

    middle = list(range(soon, pieces - direct))
    tail = list(range(pieces - direct, pieces))
    split = len(middle) - SOON_AT
    order = middle[:TAIL_AT] + tail + middle[TAIL_AT:split] + list(range(soon)) + middle[split:]
    ends = middle + list(range(soon)) + tail
    ready = [soon]
    for i in range(pieces):
        ready.append(ready[-1])
        while ready[-1] in order[:i + 1]:
            ready[-1] += 1

    def look(table, i):
        value = table[0] + i * (table[1] - table[0])
        for j in range(1, len(table) - 1):
            if table[j + 1] - table[j] != table[j] - table[j - 1] or j == len(table) - 2:
                value = jnp.where(i >= j, table[j] + (i - j) * (table[j + 1] - table[j]), value)
        return value

    def place_of(p):
        at = p - soon + jnp.where(p < soon, pieces, 0)
        return at // heads, at % heads

    def chained(i):
        return look(order, i)

    def slot(c):
        return handed + c * (1 - 2 * handed)

    barrier = pltpu.get_barrier_semaphore()

    @pl.when(s > 0)
    def _():
        pl.semaphore_signal(barrier, inc=1, device_id=(r, (s + n - 1) % n), device_id_type=MESH)

    @pl.when(s < n - 1)
    def _():
        pl.semaphore_signal(barrier, inc=1, device_id=(r, n - 1), device_id_type=MESH)

    pl.semaphore_signal(barrier, inc=1, device_id=(partner, s), device_id_type=MESH)
    loads = [
        pltpu.make_async_copy(src, dst, load_sem.at[i])
        for i, (src, dst) in enumerate(
            ((k_hbm, k_ref), (v_hbm, v_ref), (q_hbm, q_ref), (do_hbm, do_ref))
        )
    ]
    for load in loads:
        load.start()

    @pl.when(s == n - 1)
    def _():
        pl.semaphore_wait(barrier, n)
        for t in range(n - 2):
            pl.semaphore_signal(far, inc=1, device_id=(r, t), device_id_type=MESH)

    loads[0].wait()
    loads[1].wait()

    for c in range(2):
        epbuf[s, c:c + 1, 0:rows] = jnp.where(
            slot(c) == 0, ep_ref[0:1, :], ep_ref[1:2, :]
        )
        for g in range(heads):
            kvbuf[c, g, own, 0:DH] = k_ref[slot(c), :, g * DH:(g + 1) * DH]
            kvbuf[c, g, own, DH:2 * DH] = v_ref[slot(c), :, g * DH:(g + 1) * DH]

    @pl.when(s < n - 1)
    def _():
        pl.semaphore_wait(barrier, 2)

    def chunk(t, skip=0):
        return pl.ds(pl.multiple_of(t * rows + skip, 16), rows - skip)

    def up_own(p, t):
        part = kvbuf.at[(*place_of(p), chunk(t))]
        return pltpu.make_async_remote_copy(
            src_ref=part, dst_ref=part, send_sem=own_send, recv_sem=own_recv.at[p],
            device_id=(r, above), device_id_type=MESH,
        )

    def up_fwd(p, k):
        part = kvbuf.at[(*place_of(p), pl.ds(low(k), k * rows - low(k)))]
        return pltpu.make_async_remote_copy(
            src_ref=part, dst_ref=part, send_sem=fwd_send.at[place_of(p)[0]], recv_sem=fwd_recv.at[p],
            device_id=(r, above), device_id_type=MESH,
        )

    def up_far(p, t):
        part = kvbuf.at[(*place_of(p), chunk(t, first(n - 1 - t)))]
        return pltpu.make_async_remote_copy(
            src_ref=part, dst_ref=part, send_sem=far_send, recv_sem=far_recv.at[p, t],
            device_id=(r, n - 1), device_id_type=MESH,
        )

    def ep_far(t):
        return pltpu.make_async_remote_copy(
            src_ref=epbuf.at[t], dst_ref=epbuf.at[t],
            send_sem=ep_send.at[n - 1], recv_sem=ep_recv.at[t],
            device_id=(r, n - 1), device_id_type=MESH,
        )

    def ep_copy(t):
        return pltpu.make_async_remote_copy(
            src_ref=epbuf.at[t], dst_ref=epbuf.at[t],
            send_sem=ep_send.at[t], recv_sem=ep_recv.at[t],
            device_id=(r, above), device_id_type=MESH,
        )

    def down_sum(p):
        part = (*place_of(p), pl.ds(low(n - 2), top - low(n - 2)))
        return pltpu.make_async_remote_copy(
            src_ref=gpart.at[part], dst_ref=grecv.at[part],
            send_sem=acc_send.at[place_of(p)[0]], recv_sem=acc_recv.at[p],
            device_id=(r, (s + n - 1) % n), device_id_type=MESH,
        )

    def down(p, d):
        c, g = place_of(p)
        return pltpu.make_async_remote_copy(
            src_ref=gpart.at[c, g, chunk((s + n - d) % n, first(d))],
            dst_ref=grecv.at[c, g, chunk(s, first(d))],
            send_sem=down_send.at[d], recv_sem=down_recv.at[p, s],
            device_id=(r, (s + n - d) % n), device_id_type=MESH,
        )

    def down_arrival(p, d):
        c, g = place_of(p)
        part = grecv.at[c, g, chunk((s + d) % n, first(d))]
        return pltpu.make_async_remote_copy(
            src_ref=part, dst_ref=part,
            send_sem=down_send.at[d], recv_sem=down_recv.at[p, (s + d) % n],
            device_id=(r, (s + d) % n), device_id_type=MESH,
        )

    def send_down(p):
        for d in reversed(reach):
            @pl.when(s >= d)
            def _(d=d):
                down(p, d).start()

    def trade(which, g, buf, out, width):
        cols = pl.ds(pl.multiple_of(g * width, width), width)
        return pltpu.make_async_remote_copy(
            src_ref=buf.at[0, :, cols], dst_ref=out.at[1, :, cols],
            send_sem=trade_send.at[which], recv_sem=trade_recv.at[which],
            device_id=(partner, s), device_id_type=MESH,
        )

    def keep(which, g, buf, out, width):
        cols = pl.ds(pl.multiple_of(g * width, width), width)
        return pltpu.make_async_copy(
            buf.at[1, :, cols], out.at[0, :, cols], keep_sem.at[which]
        )

    lead = jnp.where(s == n - 2, LEAD_TOP, LEAD)

    @pl.when(s < n - 1)
    def _():
        ep_copy(s).start()

        def early(i, carry):
            up_own(jnp.where(s == n - 2, i, chained(i)), s).start()
            return carry

        lax.fori_loop(0, lead, early, 0)

    for t in range(n - 2):
        @pl.when(s == t)
        def _(t=t):
            pl.semaphore_wait(far, 1)
            ep_far(t).start()
            if n - 1 - t in reach:
                for p in range(soon):
                    up_far(p, t).start()

    @pl.when(s == 0)
    def _():
        def remaining(i, carry):
            up_own(chained(i), s).start()
            return carry

        lax.fori_loop(lead, pieces, remaining, 0)

    def clear(at, size):
        def one(i, carry):
            kvbuf[i // heads, i % heads, pl.ds(at, size), :] = (
                jnp.zeros((size, 2 * DH), jnp.bfloat16)
            )
            return carry

        lax.fori_loop(0, 2 * heads, one, 0)

    eye = lax.broadcasted_iota(jnp.int32, (rows, DH), 0) == lax.broadcasted_iota(
        jnp.int32, (rows, DH), 1
    )

    def see(t):
        def one(c, carry):
            mine = epbuf[s, pl.ds(c, 1), 0:rows]
            mine = jnp.concatenate([mine] * groups, axis=1)
            pos_q = jnp.concatenate(
                [s * rows + lax.broadcasted_iota(jnp.int32, (rows, rows), 1)] * groups, axis=1
            )
            line = epbuf[t, pl.ds(c, 1), :]
            column = jnp.sum(jnp.where(eye, line, 0), axis=1, keepdims=True)
            pos_k = t * rows + lax.broadcasted_iota(jnp.int32, (rows, wide), 0)
            seen = jnp.where(pos_k <= pos_q, 1.0, 0.0) * jnp.where(column == mine, 1.0, 0.0)
            allow[c, chunk(t), :] = seen
            return carry

        lax.fori_loop(0, 2, one, 0)

    for t in range(n):
        @pl.when(t > s)
        def _(t=t):
            clear(t * rows, rows)
            for c in range(2):
                allow[c, t * rows:(t + 1) * rows, :] = jnp.zeros((rows, wide), jnp.float32)
    for k in range(1, n):
        if low(k - 1) > 0:
            @pl.when(s == k)
            def _(k=k):
                clear(0, low(k - 1))
    see(s)
    loads[2].wait()
    loads[3].wait()

    def ep_step(d, carry):
        t = s - d
        ep_copy(t).wait_recv()

        @pl.when(s < n - 2)
        def _():
            ep_copy(t).start()
        see(t)
        return carry

    lax.fori_loop(1, s + 1, ep_step, 0)

    def forward(i):
        p = jnp.where(s == n - 1, i, chained(i))

        @pl.when(s > 0)
        def _():
            up_own(p, (s + n - 1) % n).wait_recv()
        for k in range(1, n):
            @pl.when(s == k)
            def _(k=k):
                if k == n - 1:
                    @pl.when(p < soon)
                    def _():
                        for t in range(n - 2):
                            if n - 1 - t in reach:
                                up_far(p, t).wait_recv()

                    @pl.when(p >= soon)
                    def _():
                        up_fwd(p, k - 1).wait_recv()
                elif k == n - 2:
                    up_fwd(p, k - 1).wait_recv()
                    was, now = look(ready, i), look(ready, i + 1)

                    def pass_on(f, carry):
                        up_fwd(f, k).start()

                        @pl.when(f + lead - soon < pieces)
                        def _():
                            up_own(f + lead - soon, s).start()
                        return carry

                    lax.fori_loop(was, now, pass_on, 0)
                else:
                    if k > 1:
                        up_fwd(p, k - 1).wait_recv()
                    up_fwd(p, k).start()

    def compute(p):
        c, g = place_of(p)
        at = slot(c)

        def stack(ref):
            return jnp.concatenate(
                [
                    ref[at, :, pl.ds(pl.multiple_of((g * groups + i) * DH, DH), DH)]
                    for i in range(groups)
                ],
                axis=0,
            )

        q = stack(q_ref)
        do = stack(do_ref)
        key = kvbuf[c, g, :, 0:DH]
        value = kvbuf[c, g, :, DH:2 * DH]
        scores = jnp.where(allow[c] > 0.5, dot(key, q, NT) * scaling, jnp.float32(-1e30))
        peak = jnp.max(scores, axis=0, keepdims=True)
        expo = jnp.exp(scores - peak)
        probs = expo * (1.0 / jnp.sum(expo, axis=0, keepdims=True))
        dprobs = dot(value, do, NT)
        delta = jnp.sum(probs * dprobs, axis=0, keepdims=True)
        dscores = (probs * (dprobs - delta)).astype(jnp.bfloat16)
        gk = dot(dscores, q, NN)
        gv = dot(probs.astype(jnp.bfloat16), do, NN)
        gown[c, g, :, 0:DH] = gk
        gown[c, g, :, DH:2 * DH] = gv
        gpart[c, g, :, 0:DH] = gk.astype(jnp.bfloat16)
        gpart[c, g, :, DH:2 * DH] = gv.astype(jnp.bfloat16)

        @pl.when((s == n - 1) & summed(p))
        def _():
            down_sum(p).start()
            down(p, 1).start()

        @pl.when((s < n - 2) | jnp.logical_not(summed(p)))
        def _():
            send_down(p)

        gq = (dot(dscores, key, TN) * scaling).astype(jnp.bfloat16)
        for i in range(groups):
            cols = pl.ds(pl.multiple_of((g * groups + i) * DH, DH), DH)
            tq[c, :, cols] = gq[i * rows:(i + 1) * rows]

        @pl.when(c == 0)
        def _():
            trade(0, g, tq, gq_out, groups * DH).start()

        @pl.when(c == 1)
        def _():
            keep(0, g, tq, gq_out, groups * DH).start()

    def finish(p):
        c, g = place_of(p)

        @pl.when((s == n - 2) & summed(p))
        def _():
            part = (c, g, pl.ds(low(n - 2), top - low(n - 2)))
            down_sum(p).wait_recv()
            total = gown[part] + grecv[part].astype(jnp.float32)
            gown[part] = total
            gpart[part] = total.astype(jnp.bfloat16)
            send_down(p)

        for d in reach:
            @pl.when((s + d < n - 1) | ((s + d == n - 1) & (jnp.logical_not(summed(p)) | (d == 1))))
            def _(d=d):
                down_arrival(p, d).wait_recv()
                part = (c, g, chunk(s, first(d)))
                gown[part] += grecv[c, g, chunk(s + d, first(d))].astype(jnp.float32)

        cols = pl.ds(pl.multiple_of(g * DH, DH), DH)
        tk[c, :, cols] = (gown[c, g, own, 0:DH] * scaling).astype(jnp.bfloat16)
        tv[c, :, cols] = gown[c, g, own, DH:2 * DH].astype(jnp.bfloat16)

        @pl.when(c == 0)
        def _():
            trade(1, g, tk, gk_out, DH).start()
            trade(2, g, tv, gv_out, DH).start()

        @pl.when(c == 1)
        def _():
            keep(1, g, tk, gk_out, DH).start()
            keep(2, g, tv, gv_out, DH).start()

    back = jnp.where((s == 0) | (s == n - 1), 0, jnp.where(s == n - 2, BACK_TOP, BACK))
    late = back + jnp.where(s == n - 1, 0, jnp.where(s == n - 2, LAG, pieces))

    def step(i, carry):
        @pl.when((s > 0) & (s < n - 2) & (i + lead < pieces))
        def _():
            up_own(chained(i + lead), s).start()

        @pl.when(i < pieces)
        def _():
            forward(i)

        @pl.when((i >= back) & (i < pieces + back))
        def _():
            compute(jnp.where(s == n - 1, i, chained(i - back)))

        @pl.when(i >= late)
        def _():
            finish(jnp.where(s == n - 1, i, look(ends, i - late)))
        return carry

    lax.fori_loop(0, pieces + late, step, 0)

    def sent(part, sem):
        pltpu.make_async_remote_copy(
            src_ref=part, dst_ref=part, send_sem=sem, recv_sem=sem,
            device_id=(r, above), device_id_type=MESH,
        ).wait_send()

    @pl.when(s < n - 1)
    def _():
        sent(kvbuf.at[:, :, own, :], own_send)

        def one(t, carry):
            ep_copy(t).wait_send()
            return carry

        lax.fori_loop(jnp.where(s == n - 2, s, 0), s + 1, one, 0)

    for t in range(n - 2):
        @pl.when(s == t)
        def _(t=t):
            ep_far(t).wait_send()
            if n - 1 - t in reach:
                sent(kvbuf.at[1, heads - soon:heads, chunk(t, first(n - 1 - t)), :], far_send)

    for k in range(1, n - 1):
        @pl.when(s == k)
        def _(k=k):
            held = pl.ds(low(k), k * rows - low(k))
            sent(kvbuf.at[0, :, held, :], fwd_send.at[0])
            sent(kvbuf.at[1, 0:heads - (soon if k == n - 2 else 0), held, :], fwd_send.at[1])

    for d in reach:
        @pl.when((s >= d) & (s < n - 1))
        def _(d=d):
            sent(gpart.at[:, :, chunk(s - d, first(d))], down_send.at[d])

    @pl.when(s == n - 1)
    def _():
        rest = pl.ds(low(n - 2), top - low(n - 2))
        sent(gpart.at[0, :, rest], acc_send.at[0])
        sent(gpart.at[1, 0:heads - direct - soon, rest], acc_send.at[1])
        for d in reach:
            if d == 1:
                sent(gpart.at[:, :, chunk(s - d, first(d))], down_send.at[d])
            else:
                sent(gpart.at[0, 0:soon + direct, chunk(s - d, first(d))], down_send.at[d])

    for which, buf, out in ((0, tq, gq_out), (1, tk, gk_out), (2, tv, gv_out)):
        pltpu.make_async_remote_copy(
            src_ref=buf.at[0], dst_ref=out.at[1],
            send_sem=trade_send.at[which], recv_sem=trade_recv.at[which],
            device_id=(partner, s), device_id_type=MESH,
        ).wait()
        pltpu.make_async_copy(buf.at[1], out.at[0], keep_sem.at[which]).wait()


def call(n, ndp, mask, send_slot, episodes, queries, key_rows, value_rows, cotangent):
    rows = queries.shape[1]
    heads = key_rows.shape[2] // DH
    groups = queries.shape[2] // key_rows.shape[2]
    pieces = 2 * heads
    vmem = pl.BlockSpec(memory_space=pltpu.VMEM)
    dma = pltpu.SemaphoreType.DMA
    return pl.pallas_call(
        functools.partial(kernel, n, ndp, mask),
        out_shape=[
            jax.ShapeDtypeStruct(x.shape, x.dtype) for x in (queries, key_rows, value_rows)
        ],
        in_specs=[pl.BlockSpec(memory_space=pltpu.SMEM), vmem]
        + [pl.BlockSpec(memory_space=pl.ANY)] * 4,
        out_specs=[pl.BlockSpec(memory_space=pl.ANY)] * 3,
        scratch_shapes=[
            pltpu.VMEM(queries.shape, jnp.bfloat16),
            pltpu.VMEM(key_rows.shape, jnp.bfloat16),
            pltpu.VMEM(value_rows.shape, jnp.bfloat16),
            pltpu.VMEM(cotangent.shape, jnp.bfloat16),
            dma((4,)),
            dma((3,)),
            pltpu.VMEM((2, heads, n * rows, 2 * DH), jnp.bfloat16),
            pltpu.VMEM((n, 8, DH), jnp.int32),
            pltpu.VMEM((2, n * rows, groups * rows), jnp.float32),
            pltpu.VMEM((2, heads, n * rows, 2 * DH), jnp.bfloat16),
            pltpu.VMEM((2, heads, n * rows, 2 * DH), jnp.float32),
            pltpu.VMEM((2, heads, n * rows, 2 * DH), jnp.bfloat16),
            pltpu.VMEM(queries.shape, jnp.bfloat16),
            pltpu.VMEM(key_rows.shape, jnp.bfloat16),
            pltpu.VMEM(value_rows.shape, jnp.bfloat16),
            pltpu.SemaphoreType.REGULAR,
            dma,
            dma((max(1, min(SOON, heads)), n)),
            dma,
            dma((pieces,)),
            dma((2,)),
            dma((pieces,)),
            dma((n,)),
            dma((n,)),
            dma((2,)),
            dma((pieces,)),
            dma((n,)),
            dma((pieces, n)),
            dma((3,)),
            dma((3,)),
        ],
        compiler_params=pltpu.CompilerParams(
            collective_id=mask, has_side_effects=True, vmem_limit_bytes=48 << 20
        ),
    )(send_slot, episodes, queries, key_rows, value_rows, cotangent)


def settle(*refs):
    half = len(refs) // 2
    copies = [
        pltpu.make_async_copy(src, dst, refs[-1].at[i])
        for i, (src, dst) in enumerate(zip(refs[:half], refs[half:-1]))
    ]
    for copy in copies:
        copy.start()
    for copy in copies:
        copy.wait()


def place(*grads):
    anywhere = pl.BlockSpec(memory_space=pl.ANY)
    return pl.pallas_call(
        settle,
        out_shape=[jax.ShapeDtypeStruct(x.shape, x.dtype) for x in grads],
        in_specs=[anywhere] * len(grads),
        out_specs=[anywhere] * len(grads),
        scratch_shapes=[pltpu.SemaphoreType.DMA((len(grads),))],
    )(*grads)


def solution(mesh):
    n, ndp = mesh.shape["seq"], mesh.shape["dp"]

    def per_device(queries, key_rows, value_rows, cotangent, episodes, send_slot, swap_mask):
        grads = lax.switch(
            swap_mask[0] - 1,
            [functools.partial(call, n, ndp, mask) for mask in range(1, ndp)],
            send_slot, episodes, queries, key_rows, value_rows, cotangent,
        )
        return tuple(place(*grads))

    in_specs = (
        P("dp", "seq", None),
        P("dp", "seq", None),
        P("dp", "seq", None),
        P("dp", "seq", None),
        P("dp", "seq"),
        P("dp"),
        P(),
    )
    out_specs = (P("dp", "seq", None), P("dp", "seq", None), P("dp", "seq", None))
    return jax.shard_map(
        per_device, mesh=mesh, in_specs=in_specs, out_specs=out_specs, check_vma=False
    )
```
